32 devices in a mesh: scen: 2 (over x), tm: 16 (over z, y, core).
Axes of the slice: x: 2, y: 2, z: 4, core: 2. Of those that a mesh axis runs over, the one named last changes fastest.
Arguments:
- base_injection: bfloat16 [32, 36864], P(('scen', 'tm')), parts along dimension 0, may hold values from -6 to 6
- ptdf_tiles: bfloat16 [128, 80, 128, 128], P(None, 'tm'), may hold values from -0.0625 to 0.0625
- tile_block: int32 [128, 80], P(None, 'tm'), may hold values from 0 to 17
- limits: float32 [16384], replicated, may hold values from 0.5 to 2
- stor_bus: int32 [2048], replicated, may hold values from 0 to 36863
- stor_gain: float32 [2048], replicated, may hold values from 0.5 to 4
- soc_init: float32 [32, 2048], P(('scen', 'tm')), parts along dimension 0, may hold values from 0 to 1
Outputs:
- injection: float32 [32, 36864], P(('scen', 'tm')), parts along dimension 0
- line_dual: float32 [32, 16384], P(('scen', 'tm')), parts along dimension 0
- level: float32 [32, 2048], P(('scen', 'tm')), parts along dimension 0
The draws below stay inside these ranges and needn't reach their ends.
There are 2 independent parts, one for each index of `scen`. The reference program is written for one: setup_inputs(seed, part) draws one part's arguments, and reference() takes and returns one part's arrays. A program takes and returns all parts, laid end to end along the dimension named above; an argument that names none is the same for every part. Nothing has to cross between parts.
All inputs are finite; a program needn't handle non-finite values.
Results may differ from the reference program's by a relative error of at most 0.012.
The reference program's roundings to bfloat16 on the way count: a program that leaves them out, or rounds other values in their place, can miss the bound.
Values may be sent and summed in bfloat16 or wider, within the bound.
A program may use at most 128 MiB of HBM per device.

```python
import math
import jax
import jax.numpy as jnp
from jax import lax

TILE = 128
LG = 128
BB_DEV = 18
KD = 5
STOR = 2048
ITERS = 2
HOURS = 16
LINES = 16384
BUSES = 36864
N_TM = 16


def with_ends(values, own_key, least, high):
    index_at = [jax.random.randint(jax.random.fold_in(own_key, axis), (), 0, length) for axis, length in enumerate(values.shape)]
    longest = values.shape.index(max(values.shape))
    next_to = index_at[:longest] + [(index_at[longest] + 1) % values.shape[longest]] + index_at[longest + 1:]
    return values.at[tuple(index_at)].set(least).at[tuple(next_to)].set(high)


def block_levels(own_key, extent, pieces, low, largest):
    def one(dim, parts):
        draws = jax.random.uniform(jax.random.fold_in(jax.random.fold_in(own_key, 6), dim), (parts,), jnp.float32, low / len(pieces), largest / len(pieces))
        return jnp.repeat(jnp.exp(draws), extent[dim] // parts).reshape((-1,) + (1,) * (len(extent) - dim - 1))

    level = one(*pieces[0])
    for cut in pieces[1:]:
        level = level * one(*cut)
    return level


def centred(stream_key, dims, scale, reach, shards=(), kind=jnp.bfloat16):
    entries = jax.random.normal(stream_key, dims, jnp.float32) * scale
    if len(shards) > 0:
        entries = block_levels(stream_key, dims, shards, -0.22, 0.18) * entries
    return jnp.clip(entries, min=-reach, max=reach).astype(kind)


def setup_inputs(seed: int = 0, part: int = 0) -> dict:
    splits = jax.random.split(jax.random.key(seed), 8)
    own_keys = jax.random.split(jax.random.fold_in(splits[7], part), 8)
    return {
        "base_injection": centred(own_keys[0], (HOURS, BUSES), 1.0, 6.0, ((0, 16),)),
        "ptdf_tiles": centred(splits[1], (LG, KD * N_TM, TILE, TILE), (KD * N_TM * TILE) ** -0.5, 0.0625, ((1, 16),)),
        "tile_block": with_ends(jax.random.randint(splits[2], (LG, KD * N_TM), 0, BB_DEV), jax.random.fold_in(splits[2], 1), 0, BB_DEV - 1).astype(jnp.int32),
        "limits": jnp.clip(jax.random.uniform(splits[3], (LINES,), jnp.float32, 0.5, 2.0), 0.5, 2.0),
        "stor_bus": with_ends(jax.random.randint(splits[4], (STOR,), 0, BUSES), jax.random.fold_in(splits[4], 1), 0, BUSES - 1).astype(jnp.int32),
        "stor_gain": jnp.clip(jnp.exp(jax.random.uniform(splits[5], (STOR,), jnp.float32, math.log(0.5), math.log(4.0))), 0.5, 4.0),
        "soc_init": jnp.clip(1.0 * jax.random.uniform(own_keys[6], (HOURS, STOR), jnp.float32) ** block_levels(own_keys[6], (HOURS, STOR), ((0, 16),), -0.2, 0.2), 0.0, 1.0),
    }


step_size = 0.5
penalty = 4.0
ramp_weight = 0.5


def flow_product(sent, ptdf_tiles, tile_block):
    grid = sent.astype(jnp.float32).reshape(HOURS, N_TM, BB_DEV, TILE)
    tiles = ptdf_tiles.reshape(LG, N_TM, KD, TILE, TILE)
    blocks = tile_block.reshape(LG, N_TM, KD)
    device_ids = jnp.arange(N_TM, dtype=jnp.int32)[:, None]

    def one_group(pair):
        tiles_g, blocks_g = pair
        picked = grid[:, device_ids, blocks_g]
        return jnp.einsum("hnkb,nklb->hl", picked, tiles_g.astype(jnp.float32), precision=lax.Precision.HIGHEST)

    result = lax.map(one_group, (tiles, blocks))
    return jnp.transpose(result, (1, 0, 2)).reshape(HOURS, LG * TILE)


def price_product(dual_b, ptdf_tiles, tile_block):
    folded = jnp.transpose(dual_b.astype(jnp.float32).reshape(HOURS, LG, TILE), (1, 0, 2))
    tiles = ptdf_tiles.reshape(LG, N_TM, KD, TILE, TILE)
    blocks = tile_block.reshape(LG, N_TM, KD)
    device_ids = jnp.arange(N_TM, dtype=jnp.int32)[:, None]

    def add_group(total, triple):
        rows_g, tiles_g, blocks_g = triple
        contrib = jnp.einsum("hl,nklb->hnkb", rows_g, tiles_g.astype(jnp.float32), precision=lax.Precision.HIGHEST)
        return total.at[:, device_ids, blocks_g].add(contrib), None

    start_total = jnp.zeros((HOURS, N_TM, BB_DEV, TILE), jnp.float32)
    total, unused = lax.scan(add_group, start_total, (folded, tiles, blocks))
    return total.reshape(HOURS, BB_DEV * TILE * N_TM)


def reference(base_injection, ptdf_tiles, tile_block, limits, stor_bus, stor_gain, soc_init):
    base_full = base_injection.astype(jnp.float32)
    inject = base_full
    line_dual = jnp.zeros((HOURS, LG * TILE), jnp.float32)
    level = soc_init
    for iteration in range(ITERS):
        prev_inj = jnp.roll(inject, 1, axis=0)
        next_inj = jnp.roll(inject, -1, axis=0)
        prev_level = jnp.roll(level, 1, axis=0)
        line_flows = flow_product(inject.astype(jnp.bfloat16), ptdf_tiles, tile_block)
        shifted = line_flows + line_dual
        clipped = jnp.clip(shifted, -limits, limits)
        line_dual = shifted - clipped
        bus_price = price_product(line_dual.astype(jnp.bfloat16), ptdf_tiles, tile_block)
        store_price = bus_price[:, stor_bus]
        charge = level - prev_level
        updated = inject - step_size * ((inject - base_full) + penalty * bus_price
                                        + ramp_weight * (2.0 * inject - prev_inj - next_inj))
        updated = updated.at[:, stor_bus].add(-step_size * charge)
        level = 0.5 * (level + prev_level) - stor_gain * store_price
        inject = updated
    return inject, line_dual, level
```

```python
import functools

import jax
import jax.numpy as jnp
from jax import lax
from jax.experimental import pallas as pl
from jax.experimental.pallas import tpu as pltpu
from jax.sharding import PartitionSpec as P

ITERS = 2

step_size = 0.5
penalty = 4.0
ramp_weight = 0.5

VM = pl.BlockSpec(memory_space=pltpu.VMEM)
MESH = pl.DeviceIdType.MESH


def peer(index):
    return {"tm": index}


def greet(others):
    barrier = pltpu.get_barrier_semaphore()
    for other in others:
        pl.semaphore_signal(barrier, inc=1, device_id=peer(other), device_id_type=MESH)
    pl.semaphore_wait(barrier, len(others))


def exchange_kernel(n, in_ref, out_ref, send_sem, recv_sem):
    me = lax.axis_index("tm")
    others = [lax.rem(me + k, n) for k in range(1, n)]
    greet(others)
    copies = []
    for k, other in enumerate(others):
        copy = pltpu.make_async_remote_copy(
            src_ref=in_ref.at[other],
            dst_ref=out_ref.at[me],
            send_sem=send_sem.at[k],
            recv_sem=recv_sem.at[k],
            device_id=peer(other),
            device_id_type=MESH,
        )
        copy.start()
        copies.append(copy)
    out_ref[me] = in_ref[me]
    for copy in copies:
        copy.wait()


def exchange(n, block, collective_id):
    return pl.pallas_call(
        functools.partial(exchange_kernel, n),
        out_shape=jax.ShapeDtypeStruct(block.shape, block.dtype),
        in_specs=[VM],
        out_specs=VM,
        scratch_shapes=[
            pltpu.SemaphoreType.DMA((n - 1,)),
            pltpu.SemaphoreType.DMA((n - 1,)),
        ],
        compiler_params=pltpu.CompilerParams(collective_id=collective_id, has_side_effects=True),
        name=f"exchange_{collective_id}",
    )(block)


def clip_kernel(
    n, hours, flow_ref, dual_ref, limits_ref, all_ref, own_ref,
    first_recv, first_sum, second_recv,
    pair_send, pair_recv, row_send, row_recv, out_send, out_recv, fwd_send, fwd_recv,
):
    half = n // 2
    me = lax.axis_index("tm")
    core = lax.rem(me, 2)
    spot = me // 2
    partner = me + 1 - 2 * core
    spots = [lax.rem(spot + k, half) for k in range(1, half)]
    greet([partner] + [s * 2 + core for s in spots])

    def remote(src, dst, send, recv, device):
        copy = pltpu.make_async_remote_copy(
            src_ref=src, dst_ref=dst, send_sem=send, recv_sem=recv,
            device_id=peer(device), device_id_type=MESH,
        )
        copy.start()
        return copy

    firsts = []
    for k, s in enumerate(spots + [spot]):
        firsts.append(remote(
            flow_ref.at[s, 1 - core], first_recv.at[k], pair_send.at[k], pair_recv.at[k], partner
        ))
    seconds = []
    for k, s in enumerate(spots):
        firsts[k].wait()
        first_sum[k] = (
            flow_ref[s, core].astype(jnp.float32) + first_recv[k].astype(jnp.float32)
        ).astype(jnp.bfloat16)
        seconds.append(remote(
            first_sum.at[k], second_recv.at[k], row_send.at[k], row_recv.at[k], s * 2 + core
        ))
    firsts[half - 1].wait()
    total = flow_ref[spot, core].astype(jnp.float32) + first_recv[half - 1].astype(jnp.float32)
    for k in range(half - 1):
        seconds[k].wait()
        total = total + second_recv[k].astype(jnp.float32)
    rows = total.shape[0]
    shifted = (total + dual_ref[...]).reshape(rows // hours, hours, total.shape[1])
    bound = limits_ref[...][:, None, :]
    clipped = jnp.minimum(jnp.maximum(shifted, -bound), bound)
    dual = (shifted - clipped).reshape(total.shape)
    own_ref[...] = dual
    all_ref[spot, core] = dual.astype(jnp.bfloat16)

    outs = []
    for k, s in enumerate(spots):
        outs.append(remote(
            all_ref.at[spot, core], all_ref.at[spot, core], out_send.at[k], out_recv.at[k], s * 2 + core
        ))
    forwards = [remote(
        all_ref.at[spot, core], all_ref.at[spot, core],
        fwd_send.at[half - 1], fwd_recv.at[half - 1], partner,
    )]
    for k in range(half - 1):
        outs[k].wait_recv()
        source = lax.rem(spot + half - k - 1, half)
        forwards.append(remote(
            all_ref.at[source, core], all_ref.at[source, core], fwd_send.at[k], fwd_recv.at[k], partner
        ))
    for copy in outs:
        copy.wait_send()
    for copy in forwards:
        copy.wait()


def clip_exchange(n, hours, flow, dual, limits, collective_id):
    half = n // 2
    chunk = dual.shape
    dma = pltpu.SemaphoreType.DMA
    return pl.pallas_call(
        functools.partial(clip_kernel, n, hours),
        out_shape=(
            jax.ShapeDtypeStruct((half, 2) + chunk, jnp.bfloat16),
            jax.ShapeDtypeStruct(chunk, jnp.float32),
        ),
        in_specs=[VM] * 3,
        out_specs=(VM, VM),
        scratch_shapes=[
            pltpu.VMEM((half,) + chunk, jnp.bfloat16),
            pltpu.VMEM((half - 1,) + chunk, jnp.bfloat16),
            pltpu.VMEM((half - 1,) + chunk, jnp.bfloat16),
            dma((half,)), dma((half,)),
            dma((half - 1,)), dma((half - 1,)),
            dma((half - 1,)), dma((half - 1,)),
            dma((half,)), dma((half,)),
        ],
        compiler_params=pltpu.CompilerParams(collective_id=collective_id, has_side_effects=True),
        name=f"clip_{collective_id}",
    )(flow.reshape((half, 2) + chunk), dual, limits)


def flow_kernel(block_ref, sent_ref, tiles_ref, out_ref):
    step = pl.program_id(0)
    count, depth = tiles_ref.shape[:2]
    for g in range(count):
        picked = jnp.concatenate(
            [sent_ref[block_ref[step * count + g, k]] for k in range(depth)], axis=1
        )
        wide = jnp.concatenate([tiles_ref[g, k] for k in range(depth)], axis=1)
        out_ref[g] = lax.dot_general(
            picked, wide, (((1,), (1,)), ((), ())), preferred_element_type=jnp.float32
        ).astype(out_ref.dtype)


def partial_flow(tile_block, sent, tiles, count):
    groups, depth, lines, width = tiles.shape
    blocks, hours = sent.shape[:2]
    return pl.pallas_call(
        flow_kernel,
        out_shape=jax.ShapeDtypeStruct((groups, hours, lines), jnp.bfloat16),
        grid_spec=pltpu.PrefetchScalarGridSpec(
            num_scalar_prefetch=1,
            grid=(groups // count,),
            in_specs=[
                pl.BlockSpec((blocks, hours, width), lambda i, b: (0, 0, 0)),
                pl.BlockSpec((count, depth, lines, width), lambda i, b: (i, 0, 0, 0)),
            ],
            out_specs=pl.BlockSpec((count, hours, lines), lambda i, b: (i, 0, 0)),
        ),
        name="flow",
    )(tile_block, sent, tiles)


def price_kernel(
    unit_chunk, block_ref, dual_ref, tiles_ref, base_ref, inj_ref, level_ref, gain_ref,
    unit_block_ref, unit_lane_ref, new_inj_ref, sent_ref, new_level_ref, *totals,
):
    step = pl.program_id(0)
    count, depth = tiles_ref.shape[:2]

    @pl.when(step == 0)
    def _():
        for total in totals:
            total[...] = jnp.zeros_like(total)

    for g in range(count):
        wide = jnp.concatenate([tiles_ref[g, k] for k in range(depth)], axis=1)
        part = jnp.dot(dual_ref[g], wide, preferred_element_type=jnp.float32)
        width = part.shape[1] // depth
        for k in range(depth):
            at = block_ref[step * count + g, k]
            totals[k][at] += part[:, k * width:(k + 1) * width]

    @pl.when(step == pl.num_programs(0) - 1)
    def _():
        price = totals[0][...]
        for total in totals[1:]:
            price = price + total[...]
        blocks, hours, width = price.shape
        units = level_ref.shape[1]
        flat = price.astype(jnp.bfloat16).reshape(blocks * hours, width)
        moved = jnp.zeros((blocks * hours, width), jnp.float32)
        for start in range(0, units, unit_chunk):
            span = pl.ds(start, unit_chunk)
            block = jnp.broadcast_to(unit_block_ref[:, span], (hours, unit_chunk))
            lane = unit_lane_ref[:, span]
            rows = lax.broadcasted_iota(jnp.int32, (width, unit_chunk), 0)
            chosen = jnp.where(rows == lane, 1.0, 0.0).astype(jnp.bfloat16)
            level = level_ref[:, span]
            before = pltpu.roll(level, 1, 0)
            charge = level - before
            spread = jnp.concatenate(
                [jnp.where(block == r, charge, 0.0).astype(jnp.bfloat16) for r in range(blocks)], axis=0
            )
            moved = moved + lax.dot_general(
                spread, chosen, (((1,), (1,)), ((), ())), preferred_element_type=jnp.float32
            )
            found = jnp.dot(flat, chosen, preferred_element_type=jnp.float32)
            store_price = jnp.zeros_like(level)
            for r in range(blocks):
                store_price = store_price + jnp.where(block == r, found[r * hours:(r + 1) * hours], 0.0)
            new_level_ref[:, span] = 0.5 * (level + before) - gain_ref[:, span] * store_price
        for r in range(blocks):
            inj = inj_ref[r].astype(jnp.float32)
            ramp = 2.0 * inj - pltpu.roll(inj, 1, 0) - pltpu.roll(inj, hours - 1, 0)
            updated = inj - step_size * (
                (inj - base_ref[r].astype(jnp.float32)) + penalty * price[r] + ramp_weight * ramp
            )
            updated = updated - step_size * moved[r * hours:(r + 1) * hours]
            new_inj_ref[r] = updated
            sent_ref[r] = updated.astype(jnp.bfloat16)


def price_update(tile_block, dual_all, tiles, base, inj, level, gain, unit_block, unit_lane, count):
    groups, depth, lines, width = tiles.shape
    blocks, hours = base.shape[:2]
    units = level.shape[1]
    chunk = 512 if units % 512 == 0 else units
    whole3 = pl.BlockSpec((blocks, hours, width), lambda i, b: (0, 0, 0))
    whole2 = pl.BlockSpec((hours, units), lambda i, b: (0, 0))
    line2 = pl.BlockSpec((1, units), lambda i, b: (0, 0))
    return pl.pallas_call(
        functools.partial(price_kernel, chunk),
        out_shape=(
            jax.ShapeDtypeStruct(base.shape, jnp.float32),
            jax.ShapeDtypeStruct(base.shape, jnp.bfloat16),
            jax.ShapeDtypeStruct(level.shape, jnp.float32),
        ),
        grid_spec=pltpu.PrefetchScalarGridSpec(
            num_scalar_prefetch=1,
            grid=(groups // count,),
            in_specs=[
                pl.BlockSpec((count, hours, lines), lambda i, b: (i, 0, 0)),
                pl.BlockSpec((count, depth, lines, width), lambda i, b: (i, 0, 0, 0)),
                whole3, whole3, whole2, line2, line2, line2,
            ],
            out_specs=(whole3, whole3, whole2),
            scratch_shapes=[pltpu.VMEM(base.shape, jnp.float32)] * depth,
        ),
        name="price",
    )(tile_block, dual_all, tiles, base, inj, level, gain, unit_block, unit_lane)


def shards(base_injection, ptdf_tiles, tile_block, limits, stor_bus, stor_gain, soc_init):
    n = lax.axis_size("tm")
    me = lax.axis_index("tm")
    hours = n * base_injection.shape[0]
    groups, _, lines, width = ptdf_tiles.shape
    units = soc_init.shape[1]
    unit_rows = units // width
    blocks = base_injection.shape[1] // (n * width)
    own_groups = groups // n
    count = 8

    opening = jnp.concatenate(
        [
            base_injection.reshape(n, blocks, width),
            jnp.broadcast_to(
                soc_init.astype(jnp.bfloat16).reshape(1, unit_rows, width), (n, unit_rows, width)
            ),
        ],
        axis=1,
    )
    opened = exchange(n, opening, 0)
    base = jnp.transpose(opened[:, :blocks], (1, 0, 2))
    level = opened[:, blocks:].reshape(hours, units).astype(jnp.float32)

    local_bus = stor_bus - me * (blocks * width)
    unit_block = jnp.floor_divide(local_bus, width).reshape(1, units)
    unit_lane = jnp.remainder(local_bus, width).reshape(1, units)
    gain = stor_gain.reshape(1, units)
    own_limits = lax.dynamic_slice_in_dim(limits.reshape(groups, lines), me * own_groups, own_groups, 0)

    inj, sent = base, base
    dual = jnp.zeros((own_groups * hours, lines), jnp.float32)
    for iteration in range(ITERS):
        flow = partial_flow(tile_block, sent, ptdf_tiles, count)
        dual_all, dual = clip_exchange(n, hours, flow, dual, own_limits, 1 + iteration)
        inj, sent, level = price_update(
            tile_block, dual_all.reshape(groups, hours, lines), ptdf_tiles, base, inj, level,
            gain, unit_block, unit_lane, count,
        )

    mine = (unit_block >= 0) & (unit_block < blocks)
    closing = jnp.concatenate(
        [
            jnp.transpose(inj, (1, 0, 2)),
            jnp.transpose(dual.reshape(own_groups, hours, lines), (1, 0, 2)),
            jnp.where(mine, level, 0.0).reshape(hours, unit_rows, width),
        ],
        axis=1,
    ).astype(jnp.bfloat16)
    closed = exchange(n, closing, 1 + ITERS).astype(jnp.float32)
    return (
        closed[:, :blocks].reshape(1, -1),
        closed[:, blocks:blocks + own_groups].reshape(1, -1),
        jnp.sum(closed[:, blocks + own_groups:], axis=0).reshape(1, -1),
    )


def solution(mesh):
    in_specs = (
        P(("scen", "tm"), None),
        P(None, "tm", None, None),
        P(None, "tm"),
        P(),
        P(),
        P(),
        P(("scen", "tm"), None),
    )
    out_specs = (P(("scen", "tm"), None), P(("scen", "tm"), None), P(("scen", "tm"), None))
    return jax.shard_map(shards, mesh=mesh, in_specs=in_specs, out_specs=out_specs, check_vma=False)
```

```python
import functools

import jax
import jax.numpy as jnp
from jax import lax
from jax.experimental import pallas as pl
from jax.experimental.pallas import tpu as pltpu
from jax.sharding import PartitionSpec as P

ITERS = 2
STREAMS = 4

step_size = 0.5
penalty = 4.0
ramp_weight = 0.5

VM = pl.BlockSpec(memory_space=pltpu.VMEM)
MESH = pl.DeviceIdType.MESH


def peer(index):
    return {"tm": index}


def greet(others):
    barrier = pltpu.get_barrier_semaphore()
    for other in others:
        pl.semaphore_signal(barrier, inc=1, device_id=peer(other), device_id_type=MESH)
    pl.semaphore_wait(barrier, len(others))


def opening_kernel(n, base_ref, soc_ref, base_out, soc_out, send_sem, recv_sem):
    me = lax.axis_index("tm")
    width = base_out.shape[2]
    others = [lax.rem(me + k, n) for k in range(1, n)]
    greet(others)
    copies = []
    for k, other in enumerate(others):
        for part, (src, dst) in enumerate((
            (base_ref.at[:, pl.ds(pl.multiple_of(other * width, width), width)], base_out.at[me]),
            (soc_ref, soc_out.at[me]),
        )):
            copy = pltpu.make_async_remote_copy(
                src_ref=src, dst_ref=dst,
                send_sem=send_sem.at[part, k], recv_sem=recv_sem.at[part, k],
                device_id=peer(other), device_id_type=MESH,
            )
            copy.start()
            copies.append(copy)
    base_out[me] = base_ref[:, pl.ds(pl.multiple_of(me * width, width), width)]
    soc_out[me] = soc_ref[...]
    for copy in copies:
        copy.wait()


def opening(n, base, soc):
    return pl.pallas_call(
        functools.partial(opening_kernel, n),
        out_shape=(
            jax.ShapeDtypeStruct((n, 1, base.shape[1] // n), base.dtype),
            jax.ShapeDtypeStruct((n,) + soc.shape, soc.dtype),
        ),
        in_specs=[VM] * 2,
        out_specs=(VM, VM),
        scratch_shapes=[
            pltpu.SemaphoreType.DMA((2, n - 1)),
            pltpu.SemaphoreType.DMA((2, n - 1)),
        ],
        compiler_params=pltpu.CompilerParams(collective_id=0, has_side_effects=True),
        name="opening",
    )(base, soc)


def closing_kernel(
    n, inj_ref, dual_ref, level_ref, inj_out, dual_out, level_out,
    dual_rows, level_rows, level_recv, send_sem, recv_sem,
):
    me = lax.axis_index("tm")
    reach = inj_ref.shape[2]
    span = dual_rows.shape[2]
    width = dual_ref.shape[1]
    hours = dual_rows.shape[0]
    for h in range(hours):
        for g in range(span // width):
            dual_rows[h, :, g * width:(g + 1) * width] = dual_ref[g * hours + h:g * hours + h + 1, :]
    level_rows[...] = level_ref[...].astype(level_rows.dtype)
    others = [lax.rem(me + k, n) for k in range(1, n)]
    greet(others)
    inj_here = inj_out.at[:, pl.ds(pl.multiple_of(me * reach, reach), reach)]
    dual_here = dual_out.at[:, pl.ds(pl.multiple_of(me * span, span), span)]
    copies = []
    for k, other in enumerate(others):
        for part, (src, dst) in enumerate((
            (inj_ref.at[other], inj_here),
            (dual_rows.at[other], dual_here),
            (level_rows.at[other], level_recv.at[k]),
        )):
            copy = pltpu.make_async_remote_copy(
                src_ref=src, dst_ref=dst,
                send_sem=send_sem.at[part, k], recv_sem=recv_sem.at[part, k],
                device_id=peer(other), device_id_type=MESH,
            )
            copy.start()
            copies.append(copy)
    inj_here[...] = inj_ref[me]
    dual_here[...] = dual_rows[me]
    for copy in copies:
        copy.wait()
    level = level_ref[me]
    for k in range(n - 1):
        level = level + level_recv[k].astype(jnp.float32)
    for q in range(level.shape[0]):
        level_out[:, q * width:(q + 1) * width] = level[q:q + 1]


def closing(n, inj, dual, level, collective_id):
    hours, _, reach = inj.shape
    rows, width = dual.shape
    span = rows // hours * width
    return pl.pallas_call(
        functools.partial(closing_kernel, n),
        out_shape=(
            jax.ShapeDtypeStruct((1, n * reach), jnp.float32),
            jax.ShapeDtypeStruct((1, n * span), jnp.float32),
            jax.ShapeDtypeStruct((1, level.shape[1] * level.shape[2]), jnp.float32),
        ),
        in_specs=[VM] * 3,
        out_specs=(VM, VM, VM),
        scratch_shapes=[
            pltpu.VMEM((hours, 1, span), jnp.float32),
            pltpu.VMEM(level.shape, jnp.bfloat16),
            pltpu.VMEM((n - 1,) + level.shape[1:], jnp.bfloat16),
            pltpu.SemaphoreType.DMA((3, n - 1)),
            pltpu.SemaphoreType.DMA((3, n - 1)),
        ],
        compiler_params=pltpu.CompilerParams(collective_id=collective_id, has_side_effects=True),
        name="closing",
    )(inj, dual, level)


def clip_kernel(
    n, hours, flow_ref, dual_ref, limits_ref, all_ref, own_ref,
    first_recv, first_sum, second_recv,
    pair_send, pair_recv, row_send, row_recv, out_send, out_recv, fwd_send, fwd_recv,
):
    half = n // 2
    me = lax.axis_index("tm")
    core = lax.rem(me, 2)
    spot = me // 2
    partner = me + 1 - 2 * core
    spots = [lax.rem(spot + k, half) for k in range(1, half)]
    greet([partner] + [s * 2 + core for s in spots])

    def remote(src, dst, send, recv, device):
        copy = pltpu.make_async_remote_copy(
            src_ref=src, dst_ref=dst, send_sem=send, recv_sem=recv,
            device_id=peer(device), device_id_type=MESH,
        )
        copy.start()
        return copy

    firsts = []
    for k, s in enumerate(spots + [spot]):
        firsts.append(remote(
            flow_ref.at[s, 1 - core], first_recv.at[k], pair_send.at[k], pair_recv.at[k], partner
        ))
    seconds = []
    for k, s in enumerate(spots):
        firsts[k].wait()
        first_sum[k] = (
            flow_ref[s, core] + first_recv[k]
        ).astype(jnp.bfloat16)
        seconds.append(remote(
            first_sum.at[k], second_recv.at[k], row_send.at[k], row_recv.at[k], s * 2 + core
        ))
    firsts[half - 1].wait()
    total = flow_ref[spot, core] + first_recv[half - 1]
    for k in range(half - 1):
        seconds[k].wait()
        total = total + second_recv[k].astype(jnp.float32)
    rows = total.shape[0]
    shifted = (total + dual_ref[...]).reshape(rows // hours, hours, total.shape[1])
    bound = limits_ref[...][:, None, :]
    clipped = jnp.minimum(jnp.maximum(shifted, -bound), bound)
    dual = (shifted - clipped).reshape(total.shape)
    own_ref[...] = dual
    all_ref[spot, core] = dual.astype(jnp.bfloat16)

    outs = []
    for k, s in enumerate(spots):
        outs.append(remote(
            all_ref.at[spot, core], all_ref.at[spot, core], out_send.at[k], out_recv.at[k], s * 2 + core
        ))
    forwards = [remote(
        all_ref.at[spot, core], all_ref.at[spot, core],
        fwd_send.at[half - 1], fwd_recv.at[half - 1], partner,
    )]
    for k in range(half - 1):
        outs[k].wait_recv()
        source = lax.rem(spot + half - k - 1, half)
        forwards.append(remote(
            all_ref.at[source, core], all_ref.at[source, core], fwd_send.at[k], fwd_recv.at[k], partner
        ))
    for copy in outs:
        copy.wait_send()
    for copy in forwards:
        copy.wait()


def clip_exchange(n, hours, flow, dual, limits, collective_id):
    half = n // 2
    chunk = dual.shape
    dma = pltpu.SemaphoreType.DMA
    return pl.pallas_call(
        functools.partial(clip_kernel, n, hours),
        out_shape=(
            jax.ShapeDtypeStruct((half, 2) + chunk, jnp.bfloat16),
            jax.ShapeDtypeStruct(chunk, jnp.float32),
        ),
        in_specs=[VM] * 3,
        out_specs=(VM, VM),
        scratch_shapes=[
            pltpu.VMEM((half,) + chunk, jnp.float32),
            pltpu.VMEM((half - 1,) + chunk, jnp.bfloat16),
            pltpu.VMEM((half - 1,) + chunk, jnp.bfloat16),
            dma((half,)), dma((half,)),
            dma((half - 1,)), dma((half - 1,)),
            dma((half - 1,)), dma((half - 1,)),
            dma((half,)), dma((half,)),
        ],
        compiler_params=pltpu.CompilerParams(collective_id=collective_id, has_side_effects=True),
        name=f"clip_{collective_id}",
    )(flow.reshape((half, 2) + chunk), dual, limits)


def flow_kernel(block_ref, sent_ref, *refs):
    step = pl.program_id(0)
    tile_refs, out_ref = refs[:-1], refs[-1]
    each, depth = tile_refs[0].shape[:2]
    count = each * len(tile_refs)
    for g in range(count):
        picked = jnp.concatenate(
            [sent_ref[block_ref[step * count + g, k]] for k in range(depth)], axis=1
        )
        wide = jnp.concatenate([tile_refs[g // each][g % each, k] for k in range(depth)], axis=1)
        out_ref[g] = lax.dot_general(
            picked, wide, (((1,), (1,)), ((), ())), preferred_element_type=jnp.float32
        ).astype(out_ref.dtype)


def tile_specs(tiles, count):
    shape = (count // STREAMS,) + tiles.shape[1:]
    return [
        pl.BlockSpec(shape, lambda i, b, part=part: (i * STREAMS + part, 0, 0, 0))
        for part in range(STREAMS)
    ]


def partial_flow(tile_block, sent, tiles, count):
    groups, depth, lines, width = tiles.shape
    blocks, hours = sent.shape[:2]
    return pl.pallas_call(
        flow_kernel,
        out_shape=jax.ShapeDtypeStruct((groups, hours, lines), jnp.float32),
        grid_spec=pltpu.PrefetchScalarGridSpec(
            num_scalar_prefetch=1,
            grid=(groups // count,),
            in_specs=[
                pl.BlockSpec((blocks, hours, width), lambda i, b: (0, 0, 0)),
                *tile_specs(tiles, count),
            ],
            out_specs=pl.BlockSpec((count, hours, lines), lambda i, b: (i, 0, 0)),
        ),
        name="flow",
    )(tile_block, sent, *([tiles] * STREAMS))


def price_kernel(
    unit_chunk, last, depth, block_ref, dual_ref, *refs
):
    step = pl.program_id(0)
    tile_refs, refs = refs[:STREAMS], refs[STREAMS:]
    base_ref, inj_ref, level_ref, gain_ref, unit_ref, new_inj_ref, second_ref, new_level_ref = refs[:-depth]
    totals = refs[-depth:]
    each = tile_refs[0].shape[0]
    count = each * STREAMS

    @pl.when(step == 0)
    def _():
        for total in totals:
            total[...] = jnp.zeros_like(total)

    for g in range(count):
        wide = jnp.concatenate([tile_refs[g // each][g % each, k] for k in range(depth)], axis=1)
        part = jnp.dot(dual_ref[g], wide, preferred_element_type=jnp.float32)
        width = part.shape[1] // depth
        for k in range(depth):
            at = block_ref[step * count + g, k]
            totals[k][at] += part[:, k * width:(k + 1) * width]

    @pl.when(step == pl.num_programs(0) - 1)
    def _():
        price = totals[0][...]
        for total in totals[1:]:
            price = price + total[...]
        blocks, hours, width = price.shape
        units = level_ref.shape[1]
        flat = price.astype(jnp.bfloat16).reshape(blocks * hours, width)
        moved = jnp.zeros((blocks * hours, width), jnp.float32)
        for start in range(0, units, unit_chunk):
            span = pl.ds(start, unit_chunk)
            bus = unit_ref[:, span]
            first = lax.axis_index("tm") * blocks
            block = jnp.broadcast_to(lax.div(bus, width) - first, (hours, unit_chunk))
            lane = lax.rem(bus, width)
            rows = lax.broadcasted_iota(jnp.int32, (width, unit_chunk), 0)
            chosen = jnp.where(rows == lane, 1.0, 0.0).astype(jnp.bfloat16)
            level = level_ref[:, span]
            before = pltpu.roll(level, 1, 0)
            charge = level - before
            spread = jnp.concatenate(
                [jnp.where(block == r, charge, 0.0).astype(jnp.bfloat16) for r in range(blocks)], axis=0
            )
            moved = moved + lax.dot_general(
                spread, chosen, (((1,), (1,)), ((), ())), preferred_element_type=jnp.float32
            )
            found = jnp.dot(flat, chosen, preferred_element_type=jnp.float32)
            store_price = jnp.zeros_like(level)
            for r in range(blocks):
                store_price = store_price + jnp.where(block == r, found[r * hours:(r + 1) * hours], 0.0)
            new_level = 0.5 * (level + before) - gain_ref[:, span] * store_price
            if last:
                new_level = jnp.where((block >= 0) & (block < blocks), new_level, 0.0)
                for q in range(unit_chunk // width):
                    new_level_ref[:, start // width + q, :] = new_level[:, q * width:(q + 1) * width]
            else:
                new_level_ref[:, span] = new_level
        for r in range(blocks):
            inj = inj_ref[r].astype(jnp.float32)
            ramp = 2.0 * inj - pltpu.roll(inj, 1, 0) - pltpu.roll(inj, hours - 1, 0)
            updated = inj - step_size * (
                (inj - base_ref[r].astype(jnp.float32)) + penalty * price[r] + ramp_weight * ramp
            )
            updated = updated - step_size * moved[r * hours:(r + 1) * hours]
            if last:
                for h in range(hours):
                    new_inj_ref[h, :, r * width:(r + 1) * width] = updated[h:h + 1]
            else:
                new_inj_ref[r] = updated
                second_ref[r] = updated.astype(jnp.bfloat16)
        if last:
            second_ref[...] = jnp.zeros_like(second_ref)


def price_update(last, tile_block, dual_all, tiles, base, inj, level, gain, unit_bus, count):
    groups, depth, lines, width = tiles.shape
    blocks, hours = base.shape[:2]
    units = level.shape[1]
    chunk = 512 if units % 512 == 0 else units
    whole3 = pl.BlockSpec((blocks, hours, width), lambda i, b: (0, 0, 0))
    whole2 = pl.BlockSpec((hours, units), lambda i, b: (0, 0))
    line2 = pl.BlockSpec((1, units), lambda i, b: (0, 0))
    if last:
        outs = (
            ((hours, 1, blocks * width), jnp.float32),
            ((8, 128), jnp.float32),
            ((hours, units // width, width), jnp.float32),
        )
    else:
        outs = ((base.shape, jnp.float32), (base.shape, jnp.bfloat16), (level.shape, jnp.float32))
    return pl.pallas_call(
        functools.partial(price_kernel, chunk, last, depth),
        out_shape=tuple(jax.ShapeDtypeStruct(*out) for out in outs),
        grid_spec=pltpu.PrefetchScalarGridSpec(
            num_scalar_prefetch=1,
            grid=(groups // count,),
            in_specs=[
                pl.BlockSpec((count, hours, lines), lambda i, b: (i, 0, 0)),
                *tile_specs(tiles, count),
                whole3, whole3, whole2, line2, line2,
            ],
            out_specs=tuple(
                pl.BlockSpec(shape, lambda i, b, rank=len(shape): (0,) * rank) for shape, _ in outs
            ),
            scratch_shapes=[pltpu.VMEM(base.shape, jnp.float32)] * depth,
        ),
        name="price",
    )(tile_block, dual_all, *([tiles] * STREAMS), base, inj, level, gain, unit_bus)


def shards(base_injection, ptdf_tiles, tile_block, limits, stor_bus, stor_gain, soc_init):
    n = lax.axis_size("tm")
    me = lax.axis_index("tm")
    hours = n * base_injection.shape[0]
    groups, _, lines, width = ptdf_tiles.shape
    units = soc_init.shape[1]
    blocks = base_injection.shape[1] // (n * width)
    own_groups = groups // n
    count = 32

    base, level = opening(n, base_injection, soc_init)
    base = jnp.transpose(base.reshape(hours, blocks, width), (1, 0, 2))
    level = level.reshape(hours, units)

    unit_bus = stor_bus.reshape(1, units)
    gain = stor_gain.reshape(1, units)
    own_limits = lax.dynamic_slice_in_dim(limits.reshape(groups, lines), me * own_groups, own_groups, 0)

    inj, sent = base, base
    dual = jnp.zeros((own_groups * hours, lines), jnp.float32)
    for iteration in range(ITERS):
        flow = partial_flow(tile_block, sent, ptdf_tiles, count)
        dual_all, dual = clip_exchange(n, hours, flow, dual, own_limits, 1 + iteration)
        inj, sent, level = price_update(
            iteration == ITERS - 1, tile_block, dual_all.reshape(groups, hours, lines), ptdf_tiles,
            base, inj, level, gain, unit_bus, count,
        )
    return closing(n, inj, dual, level, 1 + ITERS)


def solution(mesh):
    in_specs = (
        P(("scen", "tm"), None),
        P(None, "tm", None, None),
        P(None, "tm"),
        P(),
        P(),
        P(),
        P(("scen", "tm"), None),
    )
    out_specs = (P(("scen", "tm"), None), P(("scen", "tm"), None), P(("scen", "tm"), None))
    return jax.shard_map(shards, mesh=mesh, in_specs=in_specs, out_specs=out_specs, check_vma=False)
```

```python
import functools

import jax
import jax.numpy as jnp
from jax import lax
from jax.experimental import pallas as pl
from jax.experimental.pallas import tpu as pltpu
from jax.sharding import PartitionSpec as P

ITERS = 2
STREAMS = 4

step_size = 0.5
penalty = 4.0
ramp_weight = 0.5

VM = pl.BlockSpec(memory_space=pltpu.VMEM)
MESH = pl.DeviceIdType.MESH


def peer(index):
    return {"tm": index}


def greet(others):
    barrier = pltpu.get_barrier_semaphore()
    for other in others:
        pl.semaphore_signal(barrier, inc=1, device_id=peer(other), device_id_type=MESH)
    pl.semaphore_wait(barrier, len(others))


def opening_kernel(n, base_ref, soc_ref, base_out, soc_out, send_sem, recv_sem):
    me = lax.axis_index("tm")
    width = base_out.shape[2]
    others = [lax.rem(me + k, n) for k in range(1, n)]
    greet(others)
    copies = []
    for k, other in enumerate(others):
        for part, (src, dst) in enumerate((
            (base_ref.at[:, pl.ds(pl.multiple_of(other * width, width), width)], base_out.at[me]),
            (soc_ref, soc_out.at[me]),
        )):
            copy = pltpu.make_async_remote_copy(
                src_ref=src, dst_ref=dst,
                send_sem=send_sem.at[part, k], recv_sem=recv_sem.at[part, k],
                device_id=peer(other), device_id_type=MESH,
            )
            copy.start()
            copies.append(copy)
    base_out[me] = base_ref[:, pl.ds(pl.multiple_of(me * width, width), width)]
    soc_out[me] = soc_ref[...]
    for copy in copies:
        copy.wait()


def opening(n, base, soc):
    return pl.pallas_call(
        functools.partial(opening_kernel, n),
        out_shape=(
            jax.ShapeDtypeStruct((n, 1, base.shape[1] // n), base.dtype),
            jax.ShapeDtypeStruct((n,) + soc.shape, soc.dtype),
        ),
        in_specs=[VM] * 2,
        out_specs=(VM, VM),
        scratch_shapes=[
            pltpu.SemaphoreType.DMA((2, n - 1)),
            pltpu.SemaphoreType.DMA((2, n - 1)),
        ],
        compiler_params=pltpu.CompilerParams(collective_id=0, has_side_effects=True),
        name="opening",
    )(base, soc)


def closing_kernel(
    n, inj_ref, dual_ref, level_ref, inj_out, dual_out, level_out,
    dual_rows, level_rows, level_recv, send_sem, recv_sem,
):
    me = lax.axis_index("tm")
    reach = inj_ref.shape[2]
    span = dual_rows.shape[2]
    width = dual_ref.shape[1]
    hours = dual_rows.shape[0]
    for h in range(hours):
        for g in range(span // width):
            dual_rows[h, :, g * width:(g + 1) * width] = dual_ref[g * hours + h:g * hours + h + 1, :]
    level_rows[...] = level_ref[...].astype(level_rows.dtype)
    others = [lax.rem(me + k, n) for k in range(1, n)]
    greet(others)
    inj_here = inj_out.at[:, pl.ds(pl.multiple_of(me * reach, reach), reach)]
    dual_here = dual_out.at[:, pl.ds(pl.multiple_of(me * span, span), span)]
    copies = []
    for k, other in enumerate(others):
        for part, (src, dst) in enumerate((
            (inj_ref.at[other], inj_here),
            (dual_rows.at[other], dual_here),
            (level_rows.at[other], level_recv.at[k]),
        )):
            copy = pltpu.make_async_remote_copy(
                src_ref=src, dst_ref=dst,
                send_sem=send_sem.at[part, k], recv_sem=recv_sem.at[part, k],
                device_id=peer(other), device_id_type=MESH,
            )
            copy.start()
            copies.append(copy)
    inj_here[...] = inj_ref[me]
    dual_here[...] = dual_rows[me]
    for copy in copies:
        copy.wait()
    level = level_ref[me]
    for k in range(n - 1):
        level = level + level_recv[k].astype(jnp.float32)
    for q in range(level.shape[0]):
        level_out[:, q * width:(q + 1) * width] = level[q:q + 1]


def closing(n, inj, dual, level, collective_id):
    hours, _, reach = inj.shape
    rows, width = dual.shape
    span = rows // hours * width
    return pl.pallas_call(
        functools.partial(closing_kernel, n),
        out_shape=(
            jax.ShapeDtypeStruct((1, n * reach), jnp.float32),
            jax.ShapeDtypeStruct((1, n * span), jnp.float32),
            jax.ShapeDtypeStruct((1, level.shape[1] * level.shape[2]), jnp.float32),
        ),
        in_specs=[VM] * 3,
        out_specs=(VM, VM, VM),
        scratch_shapes=[
            pltpu.VMEM((hours, 1, span), jnp.float32),
            pltpu.VMEM(level.shape, jnp.bfloat16),
            pltpu.VMEM((n - 1,) + level.shape[1:], jnp.bfloat16),
            pltpu.SemaphoreType.DMA((3, n - 1)),
            pltpu.SemaphoreType.DMA((3, n - 1)),
        ],
        compiler_params=pltpu.CompilerParams(collective_id=collective_id, has_side_effects=True),
        name="closing",
    )(inj, dual, level)


def flow_clip_kernel(
    n, hours, block_ref, sent_ref, dual_ref, limits_ref, tiles_ref, all_ref, own_ref,
    held, theirs, mine, first_recv, first_sum, second_recv,
    tile_sem, pair_send, pair_recv, row_send, row_recv,
    far_send, far_recv, mid_send, mid_recv, near_send, near_recv,
):
    half, quarter = n // 2, n // 4
    me = lax.axis_index("tm")
    core = lax.rem(me, 2)
    spot = me // 2
    partner = me + 1 - 2 * core
    slots, own_groups, depth = held.shape[:3]
    spots = [lax.rem(spot + k, half) for k in range(1, half)]

    def remote(src, dst, send, recv, device):
        return pltpu.make_async_remote_copy(
            src_ref=src, dst_ref=dst, send_sem=send, recv_sem=recv,
            device_id=peer(device), device_id_type=MESH,
        )

    def owner(k, other):
        return lax.rem(spot + k + 1, half) * 2 + (1 - core if other else core)

    def fetch(k, other, slot):
        return pltpu.make_async_copy(
            tiles_ref.at[pl.ds(owner(k, other) * own_groups, own_groups)], held.at[slot], tile_sem.at[slot]
        )

    def product(k, other, slot, out):
        first = owner(k, other) * own_groups
        for g in range(own_groups):
            picked = jnp.concatenate([sent_ref[block_ref[first + g, t]] for t in range(depth)], axis=1)
            wide = jnp.concatenate([held[slot, g, t] for t in range(depth)], axis=1)
            out[k, g * hours:(g + 1) * hours] = lax.dot_general(
                picked, wide, (((1,), (1,)), ((), ())), preferred_element_type=jnp.float32
            )

    def pair(k):
        return remote(theirs.at[k], first_recv.at[k], pair_send.at[k], pair_recv.at[k], partner)

    def row(k):
        return remote(
            first_sum.at[k], second_recv.at[k], row_send.at[k], row_recv.at[k],
            lax.rem(spot + k + 1, half) * 2 + core,
        )

    ahead = slots // 2
    for k in range(ahead):
        fetch(k, True, 2 * k).start()
        fetch(k, False, 2 * k + 1).start()
    greet([partner] + [s * 2 + core for s in spots])

    def pass_on(k):
        pair(k).wait_recv()
        first_sum[k] = (mine[k] + first_recv[k]).astype(jnp.bfloat16)
        row(k).start()

    def step(k, carry):
        slot = lax.rem(k, ahead) * 2
        for other, out in ((True, theirs), (False, mine)):
            place = slot if other else slot + 1
            fetch(k, other, place).wait()
            product(k, other, place, out)
            if other:
                pair(k).start()

            @pl.when(k + ahead < half)
            def _():
                fetch(k + ahead, other, place).start()

        @pl.when(k >= 1)
        def _():
            pass_on(k - 1)

        return carry

    lax.fori_loop(0, half, step, 0)
    pair(half - 1).wait_recv()
    total = mine[half - 1] + first_recv[half - 1]
    for k in range(half - 1):
        row(k).wait_recv()
        total = total + second_recv[k].astype(jnp.float32)
    rows = total.shape[0]
    shifted = (total + dual_ref[...]).reshape(rows // hours, hours, total.shape[1])
    bound = limits_ref[...][:, None, :]
    clipped = jnp.minimum(jnp.maximum(shifted, -bound), bound)
    dual = (shifted - clipped).reshape(total.shape)
    own_ref[...] = dual
    all_ref[me] = dual.astype(jnp.bfloat16)

    far, lane = me // 4, lax.rem(me, 4)
    across = me + 2 - 4 * lax.rem(me // 2, 2)
    copies = []

    def send(chunk, sends, recvs, k, device):
        copy = remote(all_ref.at[chunk], all_ref.at[chunk], sends.at[k], recvs.at[k], device)
        copy.start()
        copies.append(copy)
        return copy

    fars = [
        send(me, far_send, far_recv, k, lax.rem(far + k + 1, quarter) * 4 + lane) for k in range(quarter - 1)
    ]
    mids = [send(me, mid_send, mid_recv, 0, across)]
    send(me, near_send, near_recv, 0, partner)
    for k in range(quarter - 1):
        fars[k].wait_recv()
        source = lax.rem(far + quarter - k - 1, quarter) * 4
        mids.append(send(source + lane, mid_send, mid_recv, k + 1, across))
        send(source + lane, near_send, near_recv, k + 1, partner)
    nears = copies[quarter:quarter + 1] + copies[quarter + 2::2]
    for k in range(quarter):
        mids[k].wait_recv()
        source = lax.rem(far + quarter - k, quarter) * 4 + lax.rem(across, 4)
        nears.append(send(source, near_send, near_recv, quarter + k, partner))
    for copy in nears:
        copy.wait_recv()
    for copy in copies:
        copy.wait_send()
    for k in range(half):
        pair(k).wait_send()
    for k in range(half - 1):
        row(k).wait_send()


def flow_clip(n, tile_block, sent, dual, limits, tiles, collective_id):
    half, quarter = n // 2, n // 4
    hours = sent.shape[1]
    own_groups = tiles.shape[0] // n
    chunk = dual.shape
    slots = 4
    dma = pltpu.SemaphoreType.DMA
    return pl.pallas_call(
        functools.partial(flow_clip_kernel, n, hours),
        out_shape=(
            jax.ShapeDtypeStruct((n,) + chunk, jnp.bfloat16),
            jax.ShapeDtypeStruct(chunk, jnp.float32),
        ),
        in_specs=[pl.BlockSpec(memory_space=pltpu.SMEM)] + [VM] * 3 + [pl.BlockSpec(memory_space=pl.ANY)],
        out_specs=(VM, VM),
        scratch_shapes=[
            pltpu.VMEM((slots, own_groups) + tiles.shape[1:], tiles.dtype),
            pltpu.VMEM((half,) + chunk, jnp.float32),
            pltpu.VMEM((half,) + chunk, jnp.float32),
            pltpu.VMEM((half,) + chunk, jnp.float32),
            pltpu.VMEM((half - 1,) + chunk, jnp.bfloat16),
            pltpu.VMEM((half - 1,) + chunk, jnp.bfloat16),
            dma((slots,)),
            dma((half,)), dma((half,)),
            dma((half - 1,)), dma((half - 1,)),
            dma((quarter - 1,)), dma((quarter - 1,)),
            dma((quarter,)), dma((quarter,)),
            dma((half,)), dma((half,)),
        ],
        compiler_params=pltpu.CompilerParams(collective_id=collective_id, has_side_effects=True),
        name=f"flow_clip_{collective_id}",
    )(tile_block, sent, dual, limits, tiles)


def tile_specs(tiles, count):
    shape = (count // STREAMS,) + tiles.shape[1:]
    return [
        pl.BlockSpec(shape, lambda i, b, part=part: (i * STREAMS + part, 0, 0, 0))
        for part in range(STREAMS)
    ]


def price_kernel(
    unit_chunk, last, depth, block_ref, dual_ref, *refs
):
    step = pl.program_id(0)
    tile_refs, refs = refs[:STREAMS], refs[STREAMS:]
    base_ref, inj_ref, level_ref, gain_ref, unit_ref, new_inj_ref, second_ref, new_level_ref = refs[:-depth]
    totals = refs[-depth:]
    each = tile_refs[0].shape[0]
    count = each * STREAMS

    @pl.when(step == 0)
    def _():
        for total in totals:
            total[...] = jnp.zeros_like(total)

    for g in range(count):
        wide = jnp.concatenate([tile_refs[g // each][g % each, k] for k in range(depth)], axis=1)
        part = jnp.dot(dual_ref[g], wide, preferred_element_type=jnp.float32)
        width = part.shape[1] // depth
        for k in range(depth):
            at = block_ref[step * count + g, k]
            totals[k][at] += part[:, k * width:(k + 1) * width]

    @pl.when(step == pl.num_programs(0) - 1)
    def _():
        price = totals[0][...]
        for total in totals[1:]:
            price = price + total[...]
        blocks, hours, width = price.shape
        units = level_ref.shape[1]
        flat = price.astype(jnp.bfloat16).reshape(blocks * hours, width)
        moved = jnp.zeros((blocks * hours, width), jnp.float32)
        for start in range(0, units, unit_chunk):
            span = pl.ds(start, unit_chunk)
            bus = unit_ref[:, span]
            first = lax.axis_index("tm") * blocks
            block = jnp.broadcast_to(lax.div(bus, width) - first, (hours, unit_chunk))
            lane = lax.rem(bus, width)
            rows = lax.broadcasted_iota(jnp.int32, (width, unit_chunk), 0)
            chosen = jnp.where(rows == lane, 1.0, 0.0).astype(jnp.bfloat16)
            level = level_ref[:, span]
            before = pltpu.roll(level, 1, 0)
            charge = level - before
            spread = jnp.concatenate(
                [jnp.where(block == r, charge, 0.0).astype(jnp.bfloat16) for r in range(blocks)], axis=0
            )
            moved = moved + lax.dot_general(
                spread, chosen, (((1,), (1,)), ((), ())), preferred_element_type=jnp.float32
            )
            found = jnp.dot(flat, chosen, preferred_element_type=jnp.float32)
            store_price = jnp.zeros_like(level)
            for r in range(blocks):
                store_price = store_price + jnp.where(block == r, found[r * hours:(r + 1) * hours], 0.0)
            new_level = 0.5 * (level + before) - gain_ref[:, span] * store_price
            if last:
                new_level = jnp.where((block >= 0) & (block < blocks), new_level, 0.0)
                for q in range(unit_chunk // width):
                    new_level_ref[:, start // width + q, :] = new_level[:, q * width:(q + 1) * width]
            else:
                new_level_ref[:, span] = new_level
        for r in range(blocks):
            inj = inj_ref[r].astype(jnp.float32)
            ramp = 2.0 * inj - pltpu.roll(inj, 1, 0) - pltpu.roll(inj, hours - 1, 0)
            updated = inj - step_size * (
                (inj - base_ref[r].astype(jnp.float32)) + penalty * price[r] + ramp_weight * ramp
            )
            updated = updated - step_size * moved[r * hours:(r + 1) * hours]
            if last:
                for h in range(hours):
                    new_inj_ref[h, :, r * width:(r + 1) * width] = updated[h:h + 1]
            else:
                new_inj_ref[r] = updated
                second_ref[r] = updated.astype(jnp.bfloat16)
        if last:
            second_ref[...] = jnp.zeros_like(second_ref)


def price_update(last, tile_block, dual_all, tiles, base, inj, level, gain, unit_bus, count):
    groups, depth, lines, width = tiles.shape
    blocks, hours = base.shape[:2]
    units = level.shape[1]
    chunk = 512 if units % 512 == 0 else units
    whole3 = pl.BlockSpec((blocks, hours, width), lambda i, b: (0, 0, 0))
    whole2 = pl.BlockSpec((hours, units), lambda i, b: (0, 0))
    line2 = pl.BlockSpec((1, units), lambda i, b: (0, 0))
    if last:
        outs = (
            ((hours, 1, blocks * width), jnp.float32),
            ((8, 128), jnp.float32),
            ((hours, units // width, width), jnp.float32),
        )
    else:
        outs = ((base.shape, jnp.float32), (base.shape, jnp.bfloat16), (level.shape, jnp.float32))
    return pl.pallas_call(
        functools.partial(price_kernel, chunk, last, depth),
        out_shape=tuple(jax.ShapeDtypeStruct(*out) for out in outs),
        grid_spec=pltpu.PrefetchScalarGridSpec(
            num_scalar_prefetch=1,
            grid=(groups // count,),
            in_specs=[
                pl.BlockSpec((count, hours, lines), lambda i, b: (i, 0, 0)),
                *tile_specs(tiles, count),
                whole3, whole3, whole2, line2, line2,
            ],
            out_specs=tuple(
                pl.BlockSpec(shape, lambda i, b, rank=len(shape): (0,) * rank) for shape, _ in outs
            ),
            scratch_shapes=[pltpu.VMEM(base.shape, jnp.float32)] * depth,
        ),
        name="price",
    )(tile_block, dual_all, *([tiles] * STREAMS), base, inj, level, gain, unit_bus)


def shards(base_injection, ptdf_tiles, tile_block, limits, stor_bus, stor_gain, soc_init):
    n = lax.axis_size("tm")
    me = lax.axis_index("tm")
    hours = n * base_injection.shape[0]
    groups, _, lines, width = ptdf_tiles.shape
    units = soc_init.shape[1]
    blocks = base_injection.shape[1] // (n * width)
    own_groups = groups // n
    count = 32

    base, level = opening(n, base_injection, soc_init)
    base = jnp.transpose(base.reshape(hours, blocks, width), (1, 0, 2))
    level = level.reshape(hours, units)

    unit_bus = stor_bus.reshape(1, units)
    gain = stor_gain.reshape(1, units)
    own_limits = lax.dynamic_slice_in_dim(limits.reshape(groups, lines), me * own_groups, own_groups, 0)

    inj, sent = base, base
    dual = jnp.zeros((own_groups * hours, lines), jnp.float32)
    for iteration in range(ITERS):
        dual_all, dual = flow_clip(n, tile_block, sent, dual, own_limits, ptdf_tiles, 1 + iteration)
        inj, sent, level = price_update(
            iteration == ITERS - 1, tile_block, dual_all.reshape(groups, hours, lines), ptdf_tiles,
            base, inj, level, gain, unit_bus, count,
        )
    return closing(n, inj, dual, level, 1 + ITERS)


def solution(mesh):
    in_specs = (
        P(("scen", "tm"), None),
        P(None, "tm", None, None),
        P(None, "tm"),
        P(),
        P(),
        P(),
        P(("scen", "tm"), None),
    )
    out_specs = (P(("scen", "tm"), None), P(("scen", "tm"), None), P(("scen", "tm"), None))
    return jax.shard_map(shards, mesh=mesh, in_specs=in_specs, out_specs=out_specs, check_vma=False)
```

```python
import functools

import jax
import jax.numpy as jnp
from jax import lax
from jax.experimental import pallas as pl
from jax.experimental.pallas import tpu as pltpu
from jax.sharding import PartitionSpec as P

ITERS = 2
STREAMS = 4

step_size = 0.5
penalty = 4.0
ramp_weight = 0.5

VM = pl.BlockSpec(memory_space=pltpu.VMEM)
MESH = pl.DeviceIdType.MESH


def peer(index):
    return {"tm": index}


def greet(others):
    barrier = pltpu.get_barrier_semaphore()
    for other in others:
        pl.semaphore_signal(barrier, inc=1, device_id=peer(other), device_id_type=MESH)
    pl.semaphore_wait(barrier, len(others))


def opening_kernel(n, base_ref, out_ref, rows, wide, send_sem, recv_sem):
    me = lax.axis_index("tm")
    reach = rows.shape[2]
    blocks, _, width = out_ref.shape
    others = [lax.rem(me + k, n) for k in range(1, n)]
    greet(others)
    copies = []
    for k, other in enumerate(others):
        copy = pltpu.make_async_remote_copy(
            src_ref=base_ref.at[:, pl.ds(pl.multiple_of(other * reach, reach), reach)],
            dst_ref=rows.at[me],
            send_sem=send_sem.at[k],
            recv_sem=recv_sem.at[k],
            device_id=peer(other),
            device_id_type=MESH,
        )
        copy.start()
        copies.append(copy)
    rows[me] = base_ref[:, pl.ds(pl.multiple_of(me * reach, reach), reach)]
    for copy in copies:
        copy.wait()
    for h in range(n):
        row = rows[h].astype(jnp.float32)
        for b in range(blocks):
            wide[b, h:h + 1, :] = row[:, b * width:(b + 1) * width]
    out_ref[...] = wide[...].astype(out_ref.dtype)


def opening(n, base, width):
    reach = base.shape[1] // n
    shape = (reach // width, n, width)
    return pl.pallas_call(
        functools.partial(opening_kernel, n),
        out_shape=jax.ShapeDtypeStruct(shape, base.dtype),
        in_specs=[VM],
        out_specs=VM,
        scratch_shapes=[
            pltpu.VMEM((n, 1, reach), base.dtype),
            pltpu.VMEM(shape, jnp.float32),
            pltpu.SemaphoreType.DMA((n - 1,)),
            pltpu.SemaphoreType.DMA((n - 1,)),
        ],
        compiler_params=pltpu.CompilerParams(collective_id=0, has_side_effects=True),
        name="opening",
    )(base)


def closing_kernel(
    n, inj_ref, dual_ref, level_ref, inj_out, dual_out, level_out,
    dual_rows, level_rows, level_recv, send_sem, recv_sem,
):
    me = lax.axis_index("tm")
    reach = inj_ref.shape[2]
    span = dual_rows.shape[2]
    width = dual_ref.shape[1]
    hours = dual_rows.shape[0]
    for h in range(hours):
        for g in range(span // width):
            dual_rows[h, :, g * width:(g + 1) * width] = dual_ref[g * hours + h:g * hours + h + 1, :]
    level_rows[...] = level_ref[...].astype(level_rows.dtype)
    others = [lax.rem(me + k, n) for k in range(1, n)]
    greet(others)
    inj_here = inj_out.at[:, pl.ds(pl.multiple_of(me * reach, reach), reach)]
    dual_here = dual_out.at[:, pl.ds(pl.multiple_of(me * span, span), span)]
    copies = []
    for k, other in enumerate(others):
        for part, (src, dst) in enumerate((
            (inj_ref.at[other], inj_here),
            (dual_rows.at[other], dual_here),
            (level_rows.at[other], level_recv.at[k]),
        )):
            copy = pltpu.make_async_remote_copy(
                src_ref=src, dst_ref=dst,
                send_sem=send_sem.at[part, k], recv_sem=recv_sem.at[part, k],
                device_id=peer(other), device_id_type=MESH,
            )
            copy.start()
            copies.append(copy)
    inj_here[...] = inj_ref[me]
    dual_here[...] = dual_rows[me]
    for copy in copies:
        copy.wait()
    level = level_ref[me]
    for k in range(n - 1):
        level = level + level_recv[k].astype(jnp.float32)
    for q in range(level.shape[0]):
        level_out[:, q * width:(q + 1) * width] = level[q:q + 1]


def closing(n, inj, dual, level, collective_id):
    hours, _, reach = inj.shape
    rows, width = dual.shape
    span = rows // hours * width
    return pl.pallas_call(
        functools.partial(closing_kernel, n),
        out_shape=(
            jax.ShapeDtypeStruct((1, n * reach), jnp.float32),
            jax.ShapeDtypeStruct((1, n * span), jnp.float32),
            jax.ShapeDtypeStruct((1, level.shape[1] * level.shape[2]), jnp.float32),
        ),
        in_specs=[VM] * 3,
        out_specs=(VM, VM, VM),
        scratch_shapes=[
            pltpu.VMEM((hours, 1, span), jnp.float32),
            pltpu.VMEM(level.shape, jnp.bfloat16),
            pltpu.VMEM((n - 1,) + level.shape[1:], jnp.bfloat16),
            pltpu.SemaphoreType.DMA((3, n - 1)),
            pltpu.SemaphoreType.DMA((3, n - 1)),
        ],
        compiler_params=pltpu.CompilerParams(collective_id=collective_id, has_side_effects=True),
        name="closing",
    )(inj, dual, level)


def flow_clip_kernel(
    n, hours, opens, block_ref, sent_ref, extra_ref, limits_ref, tiles_ref, all_ref, own_ref, *refs
):
    if opens:
        level_ref, *refs = refs
        *refs, level_recv, level_send_sem, level_recv_sem = refs
    (
        held, theirs, mine, first_recv, first_sum, second_recv,
        tile_sem, pair_send, pair_recv, row_send, row_recv,
        far_send, far_recv, mid_send, mid_recv, near_send, near_recv,
    ) = refs
    half, quarter = n // 2, n // 4
    me = lax.axis_index("tm")
    core = lax.rem(me, 2)
    spot = me // 2
    partner = me + 1 - 2 * core
    slots, own_groups, depth = held.shape[:3]
    spots = [lax.rem(spot + k, half) for k in range(1, half)]

    def remote(src, dst, send, recv, device):
        return pltpu.make_async_remote_copy(
            src_ref=src, dst_ref=dst, send_sem=send, recv_sem=recv,
            device_id=peer(device), device_id_type=MESH,
        )

    def owner(k, other):
        return lax.rem(spot + k + 1, half) * 2 + (1 - core if other else core)

    def fetch(k, other, slot):
        return pltpu.make_async_copy(
            tiles_ref.at[pl.ds(owner(k, other) * own_groups, own_groups)], held.at[slot], tile_sem.at[slot]
        )

    def product(k, other, slot, out):
        first = owner(k, other) * own_groups
        for g in range(own_groups):
            picked = jnp.concatenate([sent_ref[block_ref[first + g, t]] for t in range(depth)], axis=1)
            wide = jnp.concatenate([held[slot, g, t] for t in range(depth)], axis=1)
            out[k, g * hours:(g + 1) * hours] = lax.dot_general(
                picked, wide, (((1,), (1,)), ((), ())), preferred_element_type=jnp.float32
            )

    def pair(k):
        return remote(theirs.at[k], first_recv.at[k], pair_send.at[k], pair_recv.at[k], partner)

    def row(k):
        return remote(
            first_sum.at[k], second_recv.at[k], row_send.at[k], row_recv.at[k],
            lax.rem(spot + k + 1, half) * 2 + core,
        )

    ahead = slots // 2
    for k in range(ahead):
        fetch(k, True, 2 * k).start()
        fetch(k, False, 2 * k + 1).start()
    levels = []
    if opens:
        everyone = [lax.rem(me + k, n) for k in range(1, n)]
        greet(everyone)
        for k, other in enumerate(everyone):
            copy = remote(extra_ref, level_recv.at[me], level_send_sem.at[k], level_recv_sem.at[k], other)
            copy.start()
            levels.append(copy)
        level_recv[me] = extra_ref[...]
    else:
        greet([partner] + [s * 2 + core for s in spots])

    def pass_on(k):
        pair(k).wait_recv()
        first_sum[k] = (mine[k] + first_recv[k]).astype(jnp.bfloat16)
        row(k).start()

    def step(k, carry):
        slot = lax.rem(k, ahead) * 2
        for other, out in ((True, theirs), (False, mine)):
            place = slot if other else slot + 1
            fetch(k, other, place).wait()
            product(k, other, place, out)
            if other:
                pair(k).start()

            @pl.when(k + ahead < half)
            def _():
                fetch(k + ahead, other, place).start()

        @pl.when(k >= 1)
        def _():
            pass_on(k - 1)

        return carry

    lax.fori_loop(0, half, step, 0)
    pair(half - 1).wait_recv()
    total = mine[half - 1] + first_recv[half - 1]
    for k in range(half - 1):
        row(k).wait_recv()
        total = total + second_recv[k].astype(jnp.float32)
    rows = total.shape[0]
    if not opens:
        total = total + extra_ref[...]
    shifted = total.reshape(rows // hours, hours, total.shape[1])
    bound = limits_ref[pl.ds(me * own_groups, own_groups), :][:, None, :]
    clipped = jnp.minimum(jnp.maximum(shifted, -bound), bound)
    dual = (shifted - clipped).reshape(total.shape)
    own_ref[...] = dual
    all_ref[me] = dual.astype(jnp.bfloat16)

    far, lane = me // 4, lax.rem(me, 4)
    across = me + 2 - 4 * lax.rem(me // 2, 2)
    copies = []

    def send(chunk, sends, recvs, k, device):
        copy = remote(all_ref.at[chunk], all_ref.at[chunk], sends.at[k], recvs.at[k], device)
        copy.start()
        copies.append(copy)
        return copy

    fars = [
        send(me, far_send, far_recv, k, lax.rem(far + k + 1, quarter) * 4 + lane) for k in range(quarter - 1)
    ]
    mids = [send(me, mid_send, mid_recv, 0, across)]
    send(me, near_send, near_recv, 0, partner)
    for k in range(quarter - 1):
        fars[k].wait_recv()
        source = lax.rem(far + quarter - k - 1, quarter) * 4
        mids.append(send(source + lane, mid_send, mid_recv, k + 1, across))
        send(source + lane, near_send, near_recv, k + 1, partner)
    nears = copies[quarter:quarter + 1] + copies[quarter + 2::2]
    for k in range(quarter):
        mids[k].wait_recv()
        source = lax.rem(far + quarter - k, quarter) * 4 + lax.rem(across, 4)
        nears.append(send(source, near_send, near_recv, quarter + k, partner))
    if opens:
        for copy in levels:
            copy.wait()
        for h in range(n):
            level_ref[h:h + 1, :] = level_recv[h]
    for copy in nears:
        copy.wait_recv()
    for copy in copies:
        copy.wait_send()
    for k in range(half):
        pair(k).wait_send()
    for k in range(half - 1):
        row(k).wait_send()


def flow_clip(n, tile_block, sent, extra, limits, tiles, opens, collective_id):
    half, quarter = n // 2, n // 4
    hours = sent.shape[1]
    own_groups = tiles.shape[0] // n
    chunk = (own_groups * hours, tiles.shape[2])
    slots = 4
    dma = pltpu.SemaphoreType.DMA
    outs = [
        jax.ShapeDtypeStruct((n,) + chunk, jnp.bfloat16),
        jax.ShapeDtypeStruct(chunk, jnp.float32),
    ]
    more = []
    if opens:
        outs.append(jax.ShapeDtypeStruct((n, extra.shape[1]), extra.dtype))
        more = [pltpu.VMEM((n,) + extra.shape, extra.dtype), dma((n - 1,)), dma((n - 1,))]
    return pl.pallas_call(
        functools.partial(flow_clip_kernel, n, hours, opens),
        out_shape=tuple(outs),
        in_specs=[pl.BlockSpec(memory_space=pltpu.SMEM)] + [VM] * 3 + [pl.BlockSpec(memory_space=pl.ANY)],
        out_specs=(VM,) * len(outs),
        scratch_shapes=[
            pltpu.VMEM((slots, own_groups) + tiles.shape[1:], tiles.dtype),
            pltpu.VMEM((half,) + chunk, jnp.float32),
            pltpu.VMEM((half,) + chunk, jnp.float32),
            pltpu.VMEM((half,) + chunk, jnp.float32),
            pltpu.VMEM((half - 1,) + chunk, jnp.bfloat16),
            pltpu.VMEM((half - 1,) + chunk, jnp.bfloat16),
            dma((slots,)),
            dma((half,)), dma((half,)),
            dma((half - 1,)), dma((half - 1,)),
            dma((quarter - 1,)), dma((quarter - 1,)),
            dma((quarter,)), dma((quarter,)),
            dma((half,)), dma((half,)),
        ] + more,
        compiler_params=pltpu.CompilerParams(collective_id=collective_id, has_side_effects=True),
        name=f"flow_clip_{collective_id}",
    )(tile_block, sent, extra, limits, tiles)


def tile_specs(tiles, count):
    shape = (count // STREAMS,) + tiles.shape[1:]
    return [
        pl.BlockSpec(shape, lambda i, b, part=part: (i * STREAMS + part, 0, 0, 0))
        for part in range(STREAMS)
    ]


def price_kernel(
    unit_chunk, last, depth, block_ref, dual_ref, *refs
):
    step = pl.program_id(0)
    tile_refs, refs = refs[:STREAMS], refs[STREAMS:]
    base_ref, inj_ref, level_ref, gain_ref, unit_ref, new_inj_ref, second_ref, new_level_ref = refs[:-depth]
    totals = refs[-depth:]
    each = tile_refs[0].shape[0]
    count = each * STREAMS

    @pl.when(step == 0)
    def _():
        for total in totals:
            total[...] = jnp.zeros_like(total)

    for g in range(count):
        wide = jnp.concatenate([tile_refs[g // each][g % each, k] for k in range(depth)], axis=1)
        part = jnp.dot(dual_ref[g], wide, preferred_element_type=jnp.float32)
        width = part.shape[1] // depth
        for k in range(depth):
            at = block_ref[step * count + g, k]
            totals[k][at] += part[:, k * width:(k + 1) * width]

    @pl.when(step == pl.num_programs(0) - 1)
    def _():
        price = totals[0][...]
        for total in totals[1:]:
            price = price + total[...]
        blocks, hours, width = price.shape
        units = level_ref.shape[1]
        flat = price.astype(jnp.bfloat16).reshape(blocks * hours, width)
        moved = jnp.zeros((blocks * hours, width), jnp.float32)
        for start in range(0, units, unit_chunk):
            span = pl.ds(start, unit_chunk)
            bus = unit_ref[:, span]
            first = lax.axis_index("tm") * blocks
            block = jnp.broadcast_to(lax.div(bus, width) - first, (hours, unit_chunk))
            lane = lax.rem(bus, width)
            rows = lax.broadcasted_iota(jnp.int32, (width, unit_chunk), 0)
            chosen = jnp.where(rows == lane, 1.0, 0.0).astype(jnp.bfloat16)
            level = level_ref[:, span]
            before = pltpu.roll(level, 1, 0)
            charge = level - before
            spread = jnp.concatenate(
                [jnp.where(block == r, charge, 0.0).astype(jnp.bfloat16) for r in range(blocks)], axis=0
            )
            moved = moved + lax.dot_general(
                spread, chosen, (((1,), (1,)), ((), ())), preferred_element_type=jnp.float32
            )
            found = jnp.dot(flat, chosen, preferred_element_type=jnp.float32)
            store_price = jnp.zeros_like(level)
            for r in range(blocks):
                store_price = store_price + jnp.where(block == r, found[r * hours:(r + 1) * hours], 0.0)
            new_level = 0.5 * (level + before) - gain_ref[:, span] * store_price
            if last:
                new_level = jnp.where((block >= 0) & (block < blocks), new_level, 0.0)
                for q in range(unit_chunk // width):
                    new_level_ref[:, start // width + q, :] = new_level[:, q * width:(q + 1) * width]
            else:
                new_level_ref[:, span] = new_level
        for r in range(blocks):
            inj = inj_ref[r].astype(jnp.float32)
            ramp = 2.0 * inj - pltpu.roll(inj, 1, 0) - pltpu.roll(inj, hours - 1, 0)
            updated = inj - step_size * (
                (inj - base_ref[r].astype(jnp.float32)) + penalty * price[r] + ramp_weight * ramp
            )
            updated = updated - step_size * moved[r * hours:(r + 1) * hours]
            if last:
                for h in range(hours):
                    new_inj_ref[h, :, r * width:(r + 1) * width] = updated[h:h + 1]
            else:
                new_inj_ref[r] = updated
                second_ref[r] = updated.astype(jnp.bfloat16)
        if last:
            second_ref[...] = jnp.zeros_like(second_ref)


def price_update(last, tile_block, dual_all, tiles, base, inj, level, gain, unit_bus, count):
    groups, depth, lines, width = tiles.shape
    blocks, hours = base.shape[:2]
    units = level.shape[1]
    chunk = 512 if units % 512 == 0 else units
    whole3 = pl.BlockSpec((blocks, hours, width), lambda i, b: (0, 0, 0))
    whole2 = pl.BlockSpec((hours, units), lambda i, b: (0, 0))
    line2 = pl.BlockSpec((1, units), lambda i, b: (0, 0))
    if last:
        outs = (
            ((hours, 1, blocks * width), jnp.float32),
            ((8, 128), jnp.float32),
            ((hours, units // width, width), jnp.float32),
        )
    else:
        outs = ((base.shape, jnp.float32), (base.shape, jnp.bfloat16), (level.shape, jnp.float32))
    return pl.pallas_call(
        functools.partial(price_kernel, chunk, last, depth),
        out_shape=tuple(jax.ShapeDtypeStruct(*out) for out in outs),
        grid_spec=pltpu.PrefetchScalarGridSpec(
            num_scalar_prefetch=1,
            grid=(groups // count,),
            in_specs=[
                pl.BlockSpec((count, hours, lines), lambda i, b: (i, 0, 0)),
                *tile_specs(tiles, count),
                whole3, whole3, whole2, line2, line2,
            ],
            out_specs=tuple(
                pl.BlockSpec(shape, lambda i, b, rank=len(shape): (0,) * rank) for shape, _ in outs
            ),
            scratch_shapes=[pltpu.VMEM(base.shape, jnp.float32)] * depth,
        ),
        name="price",
    )(tile_block, dual_all, *([tiles] * STREAMS), base, inj, level, gain, unit_bus)


def shards(base_injection, ptdf_tiles, tile_block, limits, stor_bus, stor_gain, soc_init):
    n = lax.axis_size("tm")
    hours = n * base_injection.shape[0]
    groups, _, lines, width = ptdf_tiles.shape
    units = soc_init.shape[1]
    count = 32

    base = opening(n, base_injection, width)
    unit_bus = stor_bus.reshape(1, units)
    gain = stor_gain.reshape(1, units)
    bounds = limits.reshape(groups, lines)

    inj, sent = base, base
    for iteration in range(ITERS):
        opens = iteration == 0
        dual_all, dual, *gathered = flow_clip(
            n, tile_block, sent, soc_init if opens else dual, bounds, ptdf_tiles, opens, 1 + iteration
        )
        if opens:
            level, = gathered
        inj, sent, level = price_update(
            iteration == ITERS - 1, tile_block, dual_all.reshape(groups, hours, lines), ptdf_tiles,
            base, inj, level, gain, unit_bus, count,
        )
    return closing(n, inj, dual, level, 1 + ITERS)


def solution(mesh):
    in_specs = (
        P(("scen", "tm"), None),
        P(None, "tm", None, None),
        P(None, "tm"),
        P(),
        P(),
        P(),
        P(("scen", "tm"), None),
    )
    out_specs = (P(("scen", "tm"), None), P(("scen", "tm"), None), P(("scen", "tm"), None))
    return jax.shard_map(shards, mesh=mesh, in_specs=in_specs, out_specs=out_specs, check_vma=False)
```
